512 devices in a mesh: pix: 64 (over x, z), frm: 8 (over y, core).
Axes of the slice: x: 4, y: 4, z: 16, core: 2. Of those that a mesh axis runs over, the one named last changes fastest.
Arguments:
- curves: bfloat16 [32768, 8192], P('pix', 'frm')
- annulus_of_block: int32 [128], P('pix'), may hold values from 0 to 3, as said below
- ref_blocks: int32 [4, 8], replicated, may hold values from 0 to 127, as said below
- keep_mask: int32 [128, 256], P('pix'), may hold values 0 or 1
- start_basis: bfloat16 [4, 32, 8192], P(None, None, 'frm'), may hold values from -6 to 6
Outputs:
- coefficients: float32 [128, 32, 256], P('pix')
The draws below stay inside these ranges and needn't reach their ends.
Inputs may be any that keep to these rules, and one draw needn't show every extreme that they name: annulus_of_block names every annulus; block b + 64 has the annulus of block b. Every entry of ref_blocks[a, :] is a block of annulus a; each list names the lowest and the highest block of its annulus; entries may repeat.
All inputs are finite; a program needn't handle non-finite values. No bound on the sum of `keep_mask` on one device may be relied on, other than what follows from the above.
Results may differ from the reference program's by a relative error of at most 0.023.
Values may be sent and summed in bfloat16 or wider, within the bound.
A program may use at most 64 MiB of HBM per device.

```python
import jax
import jax.numpy as jnp
from jax import lax

BLOCK = 256
ANNULI = 4
K = 32
RB = 8
ITERS = 4
NBLK = 128
PIXELS = 32768
FRAMES = 8192


def annulus_table(key):
    half = NBLK // 2
    first = jax.random.randint(jax.random.fold_in(key, 11), (half - ANNULI,), 0, ANNULI)
    second = jax.random.randint(jax.random.fold_in(key, 13), (half - ANNULI,), 0, ANNULI)
    extra = jnp.maximum(first, second).astype(jnp.int32)
    front = jnp.concatenate([jnp.arange(ANNULI, dtype=jnp.int32), extra])
    order = jax.random.permutation(jax.random.fold_in(key, 17), half)
    front = front[order].astype(jnp.int32)
    return jnp.concatenate([front, front])


def draw_annulus_of_block(key, part):
    return annulus_table(key)


def draw_ref_blocks(key, part):
    table = annulus_table(key)
    labels = jnp.arange(ANNULI, dtype=jnp.int32)
    ids = jnp.arange(NBLK, dtype=jnp.int32)
    member = table[None, :] == labels[:, None]
    counts = jnp.sum(member.astype(jnp.int32), axis=1)
    sort_keys = jnp.where(member, ids[None, :], NBLK + ids[None, :]).astype(jnp.int32)
    ordered = jnp.argsort(sort_keys, axis=1, stable=True).astype(jnp.int32)
    offsets = jax.random.randint(jax.random.fold_in(key, 23), (ANNULI, RB - 2), 0, counts[:, None])
    offsets = jnp.concatenate([jnp.zeros((ANNULI, 1), jnp.int32), (counts - 1)[:, None], offsets.astype(jnp.int32)], axis=1)
    return jnp.take_along_axis(ordered, offsets, axis=1).astype(jnp.int32)


def draw_curves(key, part):
    values = jax.random.normal(jax.random.fold_in(key, 43), (PIXELS, FRAMES), jnp.float32)
    return jnp.clip(values, -6.0, 6.0).astype(jnp.bfloat16)


def set_ends(result, stream_key, smallest, largest):
    shape = result.shape
    index_at = [jax.random.randint(jax.random.fold_in(stream_key, axis), (), 0, shape[axis]) for axis in range(len(shape))]
    result = result.at[tuple(index_at)].set(smallest)
    longest = shape.index(max(shape))
    index_at[longest] = (index_at[longest] + 1) % shape[longest]
    return result.at[tuple(index_at)].set(largest)


def block_levels(stream_key, dims, split, low, top_value):
    loudness, own = 1.0, jax.random.fold_in(stream_key, 6)
    for axis_at, blocks in split:
        steps = jnp.exp(jax.random.uniform(jax.random.fold_in(own, axis_at), (blocks,), jnp.float32, low / len(split), top_value / len(split)))
        loudness = loudness * jnp.repeat(steps, dims[axis_at] // blocks).reshape([-1 if axis == axis_at else 1 for axis in range(len(dims))])
    return loudness


def centred(key, shape, spread, most, split=(), kind=jnp.bfloat16):
    array = jax.random.normal(key, shape, jnp.float32) * spread
    if len(split) > 0:
        array = block_levels(key, shape, split, -0.22, 0.18) * array
    return jnp.clip(array, min=-most, max=most).astype(kind)


def setup_inputs(seed: int = 0) -> dict:
    seeds = jax.random.split(jax.random.key(seed), 6)
    return {
        "curves": draw_curves(jax.random.fold_in(seeds[5], 71), 0),
        "annulus_of_block": draw_annulus_of_block(jax.random.fold_in(seeds[5], 71), 0),
        "ref_blocks": draw_ref_blocks(jax.random.fold_in(seeds[5], 71), 0),
        "keep_mask": set_ends((jax.random.randint(seeds[3], (NBLK, BLOCK), 0, 8) < 7).astype(jnp.int32), jax.random.fold_in(seeds[3], 1), 0, 1),
        "start_basis": centred(seeds[4], (ANNULI, K, FRAMES), 1.0, 6.0, ((2, 8),)),
    }


def project_all(blocks, annulus_of_block, basis_bf):

    def one_block(pair):
        block_rows, label = pair
        chosen = basis_bf[label]
        return jnp.dot(chosen.astype(jnp.float32), block_rows.T.astype(jnp.float32), preferred_element_type=jnp.float32)
    return lax.map(one_block, (blocks, annulus_of_block))

def reference(curves, annulus_of_block, ref_blocks, keep_mask, start_basis):
    blocks = curves.reshape(NBLK, BLOCK, FRAMES)
    labels = jnp.arange(ANNULI, dtype=jnp.int32)
    member = annulus_of_block[:, None] == labels[None, :]
    global_ids = jnp.arange(NBLK, dtype=jnp.int32)
    listed = jnp.any((ref_blocks[None, :, :] == global_ids[:, None, None]) & member[:, :, None], axis=(1, 2))
    weight = (listed[:, None] & (keep_mask == 1)).astype(jnp.float32)
    basis_bf = start_basis
    for step in range(ITERS):
        proj = project_all(blocks, annulus_of_block, basis_bf) * weight[:, None, :]
        proj_bf = proj.astype(jnp.bfloat16)

        def accumulate(total, triple):
            block_rows, weights_bf, label = triple
            term = jnp.dot(weights_bf.astype(jnp.float32), block_rows.astype(jnp.float32), preferred_element_type=jnp.float32)
            return (total.at[label].add(term), None)
        span, unused = lax.scan(accumulate, jnp.zeros((ANNULI, K, FRAMES), jnp.float32), (blocks, proj_bf, annulus_of_block))
        gram = jnp.einsum('akf,ajf->akj', span, span, precision=lax.Precision.HIGHEST)
        lower = jnp.linalg.cholesky(gram)
        ortho = lax.linalg.triangular_solve(lower, span, left_side=True, lower=True)
        basis_bf = ortho.astype(jnp.bfloat16)
    return project_all(blocks, annulus_of_block, basis_bf)
```

```python
import functools

import jax
import jax.numpy as jnp
from jax import lax
from jax.experimental import pallas as pl
from jax.experimental.pallas import tpu as pltpu
from jax.sharding import PartitionSpec as P

ITERS = 4
ANNULI = 4
K = 32
NX = 4
NZ = 16
NF = 8
F32 = jnp.float32
BF16 = jnp.bfloat16
FAR_FIRST = (8, 7, 9, 6, 10, 5, 11, 4, 12, 3, 13, 2, 14, 1, 15)


def inverse_factors(gram):
    row_id = lax.broadcasted_iota(jnp.int32, (K, 128), 0)
    lane = lax.broadcasted_iota(jnp.int32, (K, 128), 1)
    first = (lane & 63) < K
    work = jnp.where(lane >= 64, jnp.where((lane & (K - 1)) == row_id, 1.0, 0.0), gram)
    scale = jnp.zeros((K, 128), F32)
    for j in range(K):
        col = jnp.where(
            first,
            jnp.broadcast_to(work[:, j : j + 1], (K, 128)),
            jnp.broadcast_to(work[:, K + j : K + j + 1], (K, 128)),
        )
        pivot = col[j : j + 1, :]
        scale = jnp.where(row_id == j, jnp.broadcast_to(lax.rsqrt(pivot), (K, 128)), scale)
        if j < K - 1:
            step = jnp.broadcast_to(work[j : j + 1, :] / pivot, (K, 128))
            work = work - jnp.where(row_id > j, col, 0.0) * step
    return work * scale


def kernel(
    ann_ref, refs_ref, keep_ref, cur_ref, sb_ref, out_ref,
    s4, xs, xr, xa, lab, zs, zr, zg, pr, gr,
    lab_s, lab_r, x1_s, x1_r, x2_s, x2_r, z1_s, z1_r, z2_s, z2_r, g_s, g_r, p_s, p_r,
):
    pix = lax.axis_index("pix")
    f = lax.axis_index("frm")
    x = pix // NZ
    z = lax.rem(pix, NZ)

    def x_peer(j):
        q = lax.rem(x + j, NX)
        return q, {"pix": q * NZ + z}

    def z_peer(j):
        q = lax.rem(z + j, NZ)
        return q, {"pix": x * NZ + q}

    def f_peer(j):
        return {"frm": lax.rem(f + j, NF)}

    def send(src, dst, s_sem, r_sem, peer):
        copy = pltpu.make_async_remote_copy(
            src_ref=src, dst_ref=dst, send_sem=s_sem, recv_sem=r_sem,
            device_id=peer, device_id_type=pl.DeviceIdType.MESH,
        )
        copy.start()
        return copy

    barrier = pltpu.get_barrier_semaphore()
    peers = [x_peer(j)[1] for j in range(1, NX)] + [z_peer(j)[1] for j in range(1, NZ)]
    peers += [f_peer(j) for j in range(1, NF)]
    for peer in peers:
        pl.semaphore_signal(barrier, inc=1, device_id=peer, device_id_type=pl.DeviceIdType.MESH)

    labels = [ann_ref[b] for b in range(2)]
    weights = []
    for b in range(2):
        hits = jnp.int32(0)
        for a in range(ANNULI):
            for r in range(8):
                same = (refs_ref[a, r] == pix * 2 + b) & (labels[b] == a)
                hits = jnp.maximum(hits, same.astype(jnp.int32))
        keep = keep_ref[b : b + 1, :]
        weights.append(jnp.where(keep == 1, jnp.full(keep.shape, hits).astype(F32), 0.0))
        lab[x, b] = jnp.full((8, 256), labels[b]).astype(F32)
        chosen = jnp.zeros((K, sb_ref.shape[2]), F32)
        for a in range(ANNULI):
            chosen = jnp.where(jnp.full(chosen.shape, labels[b]) == a, sb_ref[a].astype(F32), chosen)
        for q in range(NX):
            s4[q, K * b : K * b + K, :] = chosen[:, 256 * q : 256 * q + 256]

    pl.semaphore_wait(barrier, len(peers))
    copies = [
        send(lab.at[x], lab.at[x], lab_s.at[j - 1], lab_r.at[j - 1], x_peer(j)[1])
        for j in range(1, NX)
    ]
    for copy in copies:
        copy.wait()

    contract_last = (((1,), (1,)), ((), ()))

    def step(t, carry):
        slot = lax.rem(t, 2)
        spans = [
            jnp.concatenate([s4[q, K * b : K * b + K, :] for q in range(NX)], axis=1)
            for b in range(2)
        ]
        grams = [
            lax.dot_general(s, s, contract_last, precision=lax.Precision.HIGHEST,
                            preferred_element_type=F32)
            for s in spans
        ]
        gr[slot, f] = jnp.concatenate(grams + [jnp.zeros((K, 64), F32)], axis=1)
        g_copies = [
            send(gr.at[slot, f], gr.at[slot, f], g_s.at[slot, j - 1], g_r.at[slot, j - 1], f_peer(j))
            for j in range(1, NF)
        ]
        for b in range(2):
            high = spans[b].astype(BF16)
            low = (spans[b] - high.astype(F32)).astype(BF16)
            both = lax.dot_general(jnp.concatenate([high, low], axis=0), cur_ref[b], contract_last,
                                   preferred_element_type=F32)
            pr[slot, f, K * b : K * b + K, :] = both[:K] + both[K:]
        p_copies = [
            send(pr.at[slot, f], pr.at[slot, f], p_s.at[slot, j - 1], p_r.at[slot, j - 1], f_peer(j))
            for j in range(1, NF)
        ]
        for copy in g_copies:
            copy.wait_recv()
        gram = gr[slot, 0]
        for i in range(1, NF):
            gram = gram + gr[slot, i]
        inverse = inverse_factors(gram)
        row_id = lax.broadcasted_iota(jnp.int32, (K, 128), 0)
        lane = lax.broadcasted_iota(jnp.int32, (K, 128), 1)
        eye = jnp.where((lane & (K - 1)) == row_id, 1.0, 0.0)
        inverse = jnp.where(jnp.full((K, 128), t) == 0, eye, inverse)
        for copy in p_copies:
            copy.wait_recv()
        raw = pr[slot, 0]
        for i in range(1, NF):
            raw = raw + pr[slot, i]
        proj = [
            lax.dot_general(inverse[:, 64 + K * b : 64 + K * b + K], raw[K * b : K * b + K],
                            (((1,), (0,)), ((), ())), precision=lax.Precision.HIGHEST,
                            preferred_element_type=F32)
            for b in range(2)
        ]
        for copy in g_copies + p_copies:
            copy.wait_send()

        @pl.when(t == ITERS)
        def _():
            for b in range(2):
                out_ref[b] = proj[b]

        @pl.when(t < ITERS)
        def _():
            for b in range(2):
                masked = (proj[b] * weights[b]).astype(BF16)
                span = jnp.dot(masked, cur_ref[b], preferred_element_type=F32)
                for q in range(NX):
                    xs[q, K * b : K * b + K, :] = span[:, 256 * q : 256 * q + 256]
            copies = []
            for j in (2, 1, 3):
                q, peer = x_peer(j)
                copies.append(send(xs.at[q], xr.at[x], x1_s.at[j - 1], x1_r.at[j - 1], peer))
            xr[x] = xs[x]
            for copy in copies:
                copy.wait()
            for r in range(4):
                totals = [jnp.zeros((8, 256), F32) for _ in range(ANNULI)]
                for q in range(NX):
                    for b in range(2):
                        value = xr[q, K * b + 8 * r : K * b + 8 * r + 8, :]
                        label = lab[q, b]
                        for a in range(ANNULI):
                            totals[a] = totals[a] + jnp.where(label == a, value, 0.0)
                for a in range(ANNULI):
                    zs[4 * a + r] = totals[a]
            copies = []
            for j in FAR_FIRST:
                q, peer = z_peer(j)
                copies.append(send(zs.at[q], zr.at[z], z1_s.at[j - 1], z1_r.at[j - 1], peer))
            zr[z] = zs[z]
            for copy in copies:
                copy.wait()
            chunk = zr[0]
            for i in range(1, NZ):
                chunk = chunk + zr[i]
            zg[z] = chunk
            copies = []
            for j in FAR_FIRST:
                peer = z_peer(j)[1]
                copies.append(send(zg.at[z], zg.at[z], z2_s.at[j - 1], z2_r.at[j - 1], peer))
            for copy in copies:
                copy.wait()

            def pick(q, dst, at):
                for b in range(2):
                    label = lab[q, b]
                    for r in range(4):
                        value = jnp.zeros((8, 256), F32)
                        for a in range(ANNULI):
                            value = jnp.where(label == a, zg[4 * a + r], value)
                        dst[at, K * b + 8 * r : K * b + 8 * r + 8, :] = value

            copies = []
            for j in (2, 1, 3):
                q, peer = x_peer(j)
                pick(q, xa, q)
                copies.append(send(xa.at[q], s4.at[x], x2_s.at[j - 1], x2_r.at[j - 1], peer))
            pick(x, s4, x)
            for copy in copies:
                copy.wait()

        return carry

    lax.fori_loop(0, ITERS + 1, step, 0)


def shards(curves, annulus_of_block, ref_blocks, keep_mask, start_basis):
    nblocks = annulus_of_block.shape[0]
    frames = curves.shape[1]
    blocks = curves.reshape(nblocks, -1, frames)
    vmem = pl.BlockSpec(memory_space=pltpu.VMEM)
    smem = pl.BlockSpec(memory_space=pltpu.SMEM)
    dma = pltpu.SemaphoreType.DMA
    return pl.pallas_call(
        kernel,
        out_shape=jax.ShapeDtypeStruct((nblocks, K, blocks.shape[1]), F32),
        in_specs=[smem, smem, vmem, vmem, vmem],
        out_specs=vmem,
        scratch_shapes=[
            pltpu.VMEM((NX, 64, 256), F32),
            pltpu.VMEM((NX, 64, 256), F32),
            pltpu.VMEM((NX, 64, 256), F32),
            pltpu.VMEM((NX, 64, 256), F32),
            pltpu.VMEM((NX, 2, 8, 256), F32),
            pltpu.VMEM((NZ, 8, 256), F32),
            pltpu.VMEM((NZ, 8, 256), F32),
            pltpu.VMEM((NZ, 8, 256), F32),
            pltpu.VMEM((2, NF, 64, 256), F32),
            pltpu.VMEM((2, NF, K, 128), F32),
            dma((3,)), dma((3,)), dma((3,)), dma((3,)), dma((3,)), dma((3,)),
            dma((15,)), dma((15,)), dma((15,)), dma((15,)),
            dma((2, 7)), dma((2, 7)), dma((2, 7)), dma((2, 7)),
        ],
        compiler_params=pltpu.CompilerParams(collective_id=0, has_side_effects=True),
    )(annulus_of_block, ref_blocks, keep_mask, blocks, start_basis)


def solution(mesh):
    in_specs = (P("pix", "frm"), P("pix"), P(), P("pix", None), P(None, None, "frm"))
    out_specs = P("pix", None, None)
    return jax.shard_map(shards, mesh=mesh, in_specs=in_specs, out_specs=out_specs, check_vma=False)
```

```python
import functools

import jax
import jax.numpy as jnp
from jax import lax
from jax.experimental import pallas as pl
from jax.experimental.pallas import tpu as pltpu
from jax.sharding import PartitionSpec as P

ITERS = 4
ANNULI = 4
K = 32
NX = 4
NZ = 16
NF = 8
F32 = jnp.float32
BF16 = jnp.bfloat16
FAR_FIRST = (8, 7, 9, 6, 10, 5, 11, 4, 12, 3, 13, 2, 14, 1, 15)


def inverse_factors(gram):
    row_id = lax.broadcasted_iota(jnp.int32, (K, 128), 0)
    lane = lax.broadcasted_iota(jnp.int32, (K, 128), 1)
    first = (lane & 63) < K
    work = jnp.where(lane >= 64, jnp.where((lane & (K - 1)) == row_id, 1.0, 0.0), gram)
    scale = jnp.zeros((K, 128), F32)
    for j in range(K):
        col = jnp.where(
            first,
            jnp.broadcast_to(work[:, j : j + 1], (K, 128)),
            jnp.broadcast_to(work[:, K + j : K + j + 1], (K, 128)),
        )
        pivot = col[j : j + 1, :]
        scale = jnp.where(row_id == j, jnp.broadcast_to(lax.rsqrt(pivot), (K, 128)), scale)
        if j < K - 1:
            step = jnp.broadcast_to(work[j : j + 1, :] / pivot, (K, 128))
            work = work - jnp.where(row_id > j, col, 0.0) * step
    return work * scale


def kernel(
    ann_ref, refs_ref, keep_ref, cur_ref, sb_ref, out_ref,
    s4, xs, xr, xa, lab, zs, zr, zg, pr, gr, inv,
    lab_s, lab_r, x1_s, x1_r, x2_s, x2_r, z1_s, z1_r, z2_s, z2_r, g_s, g_r, p_s, p_r,
):
    pix = lax.axis_index("pix")
    f = lax.axis_index("frm")
    x = pix // NZ
    z = lax.rem(pix, NZ)

    def x_peer(j):
        q = lax.rem(x + j, NX)
        return q, {"pix": q * NZ + z}

    def z_peer(j):
        q = lax.rem(z + j, NZ)
        return q, {"pix": x * NZ + q}

    def f_peer(j):
        return {"frm": lax.rem(f + j, NF)}

    def send(src, dst, s_sem, r_sem, peer):
        copy = pltpu.make_async_remote_copy(
            src_ref=src, dst_ref=dst, send_sem=s_sem, recv_sem=r_sem,
            device_id=peer, device_id_type=pl.DeviceIdType.MESH,
        )
        copy.start()
        return copy

    barrier = pltpu.get_barrier_semaphore()
    peers = [x_peer(j)[1] for j in range(1, NX)] + [z_peer(j)[1] for j in range(1, NZ)]
    peers += [f_peer(j) for j in range(1, NF)]
    for peer in peers:
        pl.semaphore_signal(barrier, inc=1, device_id=peer, device_id_type=pl.DeviceIdType.MESH)

    labels = [ann_ref[b] for b in range(2)]
    weights = []
    for b in range(2):
        hits = jnp.int32(0)
        for a in range(ANNULI):
            for r in range(8):
                same = (refs_ref[a, r] == pix * 2 + b) & (labels[b] == a)
                hits = jnp.maximum(hits, same.astype(jnp.int32))
        keep = keep_ref[b : b + 1, :]
        weights.append(jnp.where(keep == 1, jnp.full(keep.shape, hits).astype(F32), 0.0))
        lab[x, b] = jnp.full((16, 256), labels[b]).astype(F32)
        chosen = jnp.zeros((K, sb_ref.shape[2]), F32)
        for a in range(ANNULI):
            chosen = jnp.where(jnp.full(chosen.shape, labels[b]) == a, sb_ref[a].astype(F32), chosen)
        for q in range(NX):
            s4[q, K * b : K * b + K, :] = chosen[:, 256 * q : 256 * q + 256].astype(BF16)

    row_id = lax.broadcasted_iota(jnp.int32, (K, 128), 0)
    lane = lax.broadcasted_iota(jnp.int32, (K, 128), 1)
    inv[...] = jnp.where((lane & (K - 1)) == row_id, 1.0, 0.0)
    pl.semaphore_wait(barrier, len(peers))
    copies = [
        send(lab.at[x], lab.at[x], lab_s.at[j - 1], lab_r.at[j - 1], x_peer(j)[1])
        for j in range(1, NX)
    ]
    for copy in copies:
        copy.wait()

    contract_last = (((1,), (1,)), ((), ()))

    def step(t, carry):
        slot = lax.rem(t, 2)
        spans = [
            jnp.concatenate([s4[q, K * b : K * b + K, :] for q in range(NX)], axis=1)
            for b in range(2)
        ]
        grams = [
            lax.dot_general(s, s, contract_last, preferred_element_type=F32) for s in spans
        ]
        gr[slot, f] = jnp.concatenate(grams + [jnp.zeros((K, 64), F32)], axis=1)
        g_copies = [
            send(gr.at[slot, f], gr.at[slot, f], g_s.at[slot, j - 1], g_r.at[slot, j - 1], f_peer(j))
            for j in range(1, NF)
        ]
        for b in range(2):
            part = lax.dot_general(spans[b], cur_ref[b], contract_last, preferred_element_type=F32)
            pr[slot, f, K * b : K * b + K, :] = part.astype(BF16)
        p_copies = [
            send(pr.at[slot, f], pr.at[slot, f], p_s.at[slot, j - 1], p_r.at[slot, j - 1], f_peer(j))
            for j in range(1, NF)
        ]
        for copy in g_copies:
            copy.wait_recv()

        @pl.when(t > 0)
        def _():
            gram = gr[slot, 0]
            for i in range(1, NF):
                gram = gram + gr[slot, i]
            inv[...] = inverse_factors(gram)

        inverse = inv[...]
        for copy in p_copies:
            copy.wait_recv()
        raw = pr[slot, 0].astype(F32)
        for i in range(1, NF):
            raw = raw + pr[slot, i].astype(F32)
        proj = [
            lax.dot_general(inverse[:, 64 + K * b : 64 + K * b + K], raw[K * b : K * b + K],
                            (((1,), (0,)), ((), ())), precision=lax.Precision.HIGHEST,
                            preferred_element_type=F32)
            for b in range(2)
        ]

        @pl.when(t == ITERS)
        def _():
            for b in range(2):
                out_ref[b] = proj[b]

        @pl.when(t < ITERS)
        def _():
            masked = [(proj[b] * weights[b]).astype(BF16) for b in range(2)]

            def quarter(q, dst, at):
                lanes = pl.ds(pl.multiple_of(q * 256, 256), 256)
                for b in range(2):
                    part = jnp.dot(masked[b], cur_ref[b, :, lanes], preferred_element_type=F32)
                    dst[at, K * b : K * b + K, :] = part.astype(BF16)

            copies = []
            for j in (2, 1, 3):
                q, peer = x_peer(j)
                quarter(q, xs, q)
                copies.append(send(xs.at[q], xr.at[x], x1_s.at[j - 1], x1_r.at[j - 1], peer))
            quarter(x, xr, x)
            for copy in copies:
                copy.wait()
            for r in range(2):
                totals = [jnp.zeros((16, 256), F32) for _ in range(ANNULI)]
                for q in range(NX):
                    for b in range(2):
                        value = xr[q, K * b + 16 * r : K * b + 16 * r + 16, :].astype(F32)
                        label = lab[q, b]
                        for a in range(ANNULI):
                            totals[a] = totals[a] + jnp.where(label == a, value, 0.0)
                for a in range(ANNULI):
                    total = totals[a].astype(BF16)
                    for h in range(2):
                        zs[4 * a + 2 * r + h] = total[:, 128 * h : 128 * h + 128]
            copies = []
            for j in FAR_FIRST:
                q, peer = z_peer(j)
                copies.append(send(zs.at[q], zr.at[z], z1_s.at[j - 1], z1_r.at[j - 1], peer))
            zr[z] = zs[z]
            for copy in copies:
                copy.wait()
            chunk = zr[0].astype(F32)
            for i in range(1, NZ):
                chunk = chunk + zr[i].astype(F32)
            zg[z] = chunk.astype(BF16)
            copies = []
            for j in FAR_FIRST:
                peer = z_peer(j)[1]
                copies.append(send(zg.at[z], zg.at[z], z2_s.at[j - 1], z2_r.at[j - 1], peer))
            for copy in copies:
                copy.wait()

            def pick(q, dst, at):
                for b in range(2):
                    for r in range(2):
                        for h in range(2):
                            label = lab[q, b, :, 128 * h : 128 * h + 128]
                            value = jnp.zeros((16, 128), F32)
                            for a in range(ANNULI):
                                value = jnp.where(label == a, zg[4 * a + 2 * r + h].astype(F32), value)
                            rows = slice(K * b + 16 * r, K * b + 16 * r + 16)
                            dst[at, rows, 128 * h : 128 * h + 128] = value.astype(BF16)

            copies = []
            for j in (2, 1, 3):
                q, peer = x_peer(j)
                pick(q, xa, q)
                copies.append(send(xa.at[q], s4.at[x], x2_s.at[j - 1], x2_r.at[j - 1], peer))
            pick(x, s4, x)
            for copy in copies:
                copy.wait()

        for copy in g_copies + p_copies:
            copy.wait_send()
        return carry

    lax.fori_loop(0, ITERS + 1, step, 0)


def shards(curves, annulus_of_block, ref_blocks, keep_mask, start_basis):
    nblocks = annulus_of_block.shape[0]
    frames = curves.shape[1]
    blocks = curves.reshape(nblocks, -1, frames)
    vmem = pl.BlockSpec(memory_space=pltpu.VMEM)
    smem = pl.BlockSpec(memory_space=pltpu.SMEM)
    dma = pltpu.SemaphoreType.DMA
    return pl.pallas_call(
        kernel,
        out_shape=jax.ShapeDtypeStruct((nblocks, K, blocks.shape[1]), F32),
        in_specs=[smem, smem, vmem, vmem, vmem],
        out_specs=vmem,
        scratch_shapes=[
            pltpu.VMEM((NX, 64, 256), BF16),
            pltpu.VMEM((NX, 64, 256), BF16),
            pltpu.VMEM((NX, 64, 256), BF16),
            pltpu.VMEM((NX, 64, 256), BF16),
            pltpu.VMEM((NX, 2, 16, 256), F32),
            pltpu.VMEM((NZ, 16, 128), BF16),
            pltpu.VMEM((NZ, 16, 128), BF16),
            pltpu.VMEM((NZ, 16, 128), BF16),
            pltpu.VMEM((2, NF, 64, 256), BF16),
            pltpu.VMEM((2, NF, K, 128), F32),
            pltpu.VMEM((K, 128), F32),
            dma((3,)), dma((3,)), dma((3,)), dma((3,)), dma((3,)), dma((3,)),
            dma((15,)), dma((15,)), dma((15,)), dma((15,)),
            dma((2, 7)), dma((2, 7)), dma((2, 7)), dma((2, 7)),
        ],
        compiler_params=pltpu.CompilerParams(collective_id=0, has_side_effects=True),
    )(annulus_of_block, ref_blocks, keep_mask, blocks, start_basis)


def solution(mesh):
    in_specs = (P("pix", "frm"), P("pix"), P(), P("pix", None), P(None, None, "frm"))
    out_specs = P("pix", None, None)
    return jax.shard_map(shards, mesh=mesh, in_specs=in_specs, out_specs=out_specs, check_vma=False)
```

```python
import functools

import jax
import jax.numpy as jnp
from jax import lax
from jax.experimental import pallas as pl
from jax.experimental.pallas import tpu as pltpu
from jax.sharding import PartitionSpec as P

ITERS = 4
ANNULI = 4
K = 32
NX = 4
NZ = 16
NF = 8
F32 = jnp.float32
BF16 = jnp.bfloat16
FRM_ORDER = (4, 3, 5, 2, 6, 1, 7)
BACK = (-4, 3, -3, 2, -2, 1, -1)
FAR_FIRST = (8, 7, 9, 6, 10, 5, 11, 4, 12, 3, 13, 2, 14, 1, 15)


def inverse_factors(gram):
    row_id = lax.broadcasted_iota(jnp.int32, (K, 128), 0)
    lane = lax.broadcasted_iota(jnp.int32, (K, 128), 1)
    first = (lane & 63) < K
    work = jnp.where(lane >= 64, jnp.where((lane & (K - 1)) == row_id, 1.0, 0.0), gram)
    scale = jnp.zeros((K, 128), F32)
    for j in range(K):
        col = jnp.where(
            first,
            jnp.broadcast_to(work[:, j : j + 1], (K, 128)),
            jnp.broadcast_to(work[:, K + j : K + j + 1], (K, 128)),
        )
        pivot = col[j : j + 1, :]
        scale = jnp.where(row_id == j, jnp.broadcast_to(lax.rsqrt(pivot), (K, 128)), scale)
        if j < K - 1:
            step = jnp.broadcast_to(work[j : j + 1, :] / pivot, (K, 128))
            work = work - jnp.where(row_id > j, col, 0.0) * step
    return work * scale


def kernel(
    ann_ref, refs_ref, keep_ref, cur_hbm, sb_hbm, out_ref,
    cur_ref, sb_ref, mk, in_s, s4, xs, xr, xa, lab, zs, zr, zg, pr, gr,
    lab_s, lab_r, x1_s, x1_r, x2_s, x2_r, z1_s, z1_r, z2_s, z2_r, g_s, g_r, p_s, p_r,
):
    pix = lax.axis_index("pix")
    f = lax.axis_index("frm")
    x = pix // NZ
    z = lax.rem(pix, NZ)

    def x_peer(j):
        q = lax.rem(x + j, NX)
        return q, {"pix": q * NZ + z}

    def z_peer(j):
        q = lax.rem(z + j, NZ)
        return q, {"pix": x * NZ + q}

    def f_peer(j):
        return {"frm": lax.rem(f + j, NF)}

    def send(src, dst, s_sem, r_sem, peer):
        copy = pltpu.make_async_remote_copy(
            src_ref=src, dst_ref=dst, send_sem=s_sem, recv_sem=r_sem,
            device_id=peer, device_id_type=pl.DeviceIdType.MESH,
        )
        copy.start()
        return copy

    barrier = pltpu.get_barrier_semaphore()
    peers = [x_peer(j)[1] for j in range(1, NX)] + [z_peer(j)[1] for j in range(1, NZ)]
    peers += [f_peer(j) for j in range(1, NF)]
    for peer in peers:
        pl.semaphore_signal(barrier, inc=1, device_id=peer, device_id_type=pl.DeviceIdType.MESH)

    sb_copy = pltpu.make_async_copy(sb_hbm, sb_ref, in_s.at[0])
    cur_copy = pltpu.make_async_copy(cur_hbm, cur_ref, in_s.at[1])
    sb_copy.start()
    cur_copy.start()

    labels = [ann_ref[b] for b in range(2)]
    weights = []
    for b in range(2):
        hits = jnp.int32(0)
        for a in range(ANNULI):
            for r in range(8):
                same = (refs_ref[a, r] == pix * 2 + b) & (labels[b] == a)
                hits = jnp.maximum(hits, same.astype(jnp.int32))
        keep = keep_ref[b : b + 1, :]
        weights.append(jnp.where(keep == 1, jnp.full(keep.shape, hits).astype(F32), 0.0))
        lab[x, b] = jnp.full((16, 256), labels[b]).astype(F32)

    contract_last = (((1,), (1,)), ((), ()))

    def project(slot, spans):
        for b in range(2):
            part = lax.dot_general(spans[b], cur_ref[b], contract_last, preferred_element_type=F32)
            pr[slot, f, K * b : K * b + K, :] = part.astype(BF16)

    def send_projection(slot):
        return [
            send(pr.at[slot, f], pr.at[slot, f], p_s.at[slot, j - 1], p_r.at[slot, j - 1], f_peer(j))
            for j in FRM_ORDER
        ]

    def sum_projection(slot):
        raw = pr[slot, 0].astype(F32)
        for i in range(1, NF):
            raw = raw + pr[slot, i].astype(F32)
        return raw

    sb_copy.wait()
    spans = []
    for b in range(2):
        chosen = jnp.zeros((K, sb_ref.shape[2]), F32)
        for a in range(ANNULI):
            chosen = jnp.where(jnp.full(chosen.shape, labels[b]) == a, sb_ref[a].astype(F32), chosen)
        spans.append(chosen.astype(BF16))
    cur_copy.wait()
    project(0, spans)
    pl.semaphore_wait(barrier, len(peers))
    copies = send_projection(0)
    lab_copies = [
        send(lab.at[x], lab.at[x], lab_s.at[j - 1], lab_r.at[j - 1], x_peer(j)[1])
        for j in range(1, NX)
    ]
    for copy in copies:
        copy.wait_recv()
    raw = sum_projection(0)
    for b in range(2):
        mk[K * b : K * b + K, :] = (raw[K * b : K * b + K] * weights[b]).astype(BF16)
    for copy in lab_copies:
        copy.wait()
    for copy in copies:
        copy.wait_send()

    def step(t, carry):
        slot = lax.rem(t, 2)
        masked = [mk[K * b : K * b + K, :] for b in range(2)]

        def quarter(q, dst, at):
            lanes = pl.ds(pl.multiple_of(q * 256, 256), 256)
            for b in range(2):
                part = jnp.dot(masked[b], cur_ref[b, :, lanes], preferred_element_type=F32)
                dst[at, K * b : K * b + K, :] = part.astype(BF16)

        copies = []
        for j in (2, 1, 3):
            q, peer = x_peer(j)
            quarter(q, xs, q)
            copies.append(send(xs.at[q], xr.at[x], x1_s.at[j - 1], x1_r.at[j - 1], peer))
        quarter(x, xr, x)
        for copy in copies:
            copy.wait()
        for r in range(2):
            totals = [jnp.zeros((16, 256), F32) for _ in range(ANNULI)]
            for q in range(NX):
                for b in range(2):
                    value = xr[q, K * b + 16 * r : K * b + 16 * r + 16, :].astype(F32)
                    label = lab[q, b]
                    for a in range(ANNULI):
                        totals[a] = totals[a] + jnp.where(label == a, value, 0.0)
            for a in range(ANNULI):
                zs[2 * a + r] = totals[a].astype(BF16)
        mine = lax.rem(z, NZ // 2)
        copies = []
        for j in FAR_FIRST:
            q, peer = z_peer(j)
            part = zs.at[lax.rem(q, NZ // 2)]
            copies.append(
                send(part, zr.at[slot, z], z1_s.at[slot, j - 1], z1_r.at[slot, j - 1], peer)
            )
        zr[slot, z] = zs[mine]
        for copy in copies:
            copy.wait_recv()
        chunk = zr[slot, 0].astype(F32)
        for i in range(1, NZ):
            chunk = chunk + zr[slot, i].astype(F32)
        zg[mine] = chunk.astype(BF16)
        back = []
        for i, j in enumerate(BACK):
            peer = z_peer(j + NZ)[1]
            back.append(send(zg.at[mine], zg.at[mine], z2_s.at[i], z2_r.at[i], peer))
        for copy in back:
            copy.wait_recv()

        def pick(q, dst, at):
            for b in range(2):
                label = lab[q, b]
                for r in range(2):
                    value = jnp.zeros((16, 256), F32)
                    for a in range(ANNULI):
                        value = jnp.where(label == a, zg[2 * a + r].astype(F32), value)
                    dst[at, K * b + 16 * r : K * b + 16 * r + 16, :] = value.astype(BF16)

        last = []
        for j in (2, 1, 3):
            q, peer = x_peer(j)
            pick(q, xa, q)
            last.append(send(xa.at[q], s4.at[x], x2_s.at[j - 1], x2_r.at[j - 1], peer))
        pick(x, s4, x)
        for copy in copies + back:
            copy.wait_send()
        for copy in last:
            copy.wait()

        spans = [
            jnp.concatenate([s4[q, K * b : K * b + K, :] for q in range(NX)], axis=1)
            for b in range(2)
        ]
        grams = [
            lax.dot_general(s, s, contract_last, preferred_element_type=F32) for s in spans
        ]
        gr[slot, f] = jnp.concatenate(
            [g[16 * r : 16 * r + 16] for g in grams for r in range(2)], axis=1
        )
        g_copies = [
            send(gr.at[slot, f], gr.at[slot, f], g_s.at[slot, j - 1], g_r.at[slot, j - 1], f_peer(j))
            for j in FRM_ORDER
        ]
        project(slot, spans)
        p_copies = send_projection(slot)
        for copy in g_copies:
            copy.wait_recv()
        gram = gr[slot, 0]
        for i in range(1, NF):
            gram = gram + gr[slot, i]
        halves = [gram[:, K * i : K * i + K] for i in range(4)]
        gram = jnp.concatenate(
            [jnp.concatenate(halves[:2], axis=0), jnp.concatenate(halves[2:], axis=0),
             jnp.zeros((K, 64), F32)], axis=1
        )
        inverse = inverse_factors(gram)
        for copy in p_copies:
            copy.wait_recv()
        raw = sum_projection(slot)
        for b in range(2):
            proj = lax.dot_general(
                inverse[:, 64 + K * b : 64 + K * b + K], raw[K * b : K * b + K],
                (((1,), (0,)), ((), ())), precision=lax.Precision.HIGHEST,
                preferred_element_type=F32,
            )
            out_ref[b] = proj
            mk[K * b : K * b + K, :] = (proj * weights[b]).astype(BF16)
        for copy in g_copies + p_copies:
            copy.wait_send()
        return carry

    lax.fori_loop(1, ITERS + 1, step, 0)


def shards(curves, annulus_of_block, ref_blocks, keep_mask, start_basis):
    nblocks = annulus_of_block.shape[0]
    frames = curves.shape[1]
    blocks = curves.reshape(nblocks, -1, frames)
    vmem = pl.BlockSpec(memory_space=pltpu.VMEM)
    hbm = pl.BlockSpec(memory_space=pl.ANY)
    smem = pl.BlockSpec(memory_space=pltpu.SMEM)
    dma = pltpu.SemaphoreType.DMA
    return pl.pallas_call(
        kernel,
        out_shape=jax.ShapeDtypeStruct((nblocks, K, blocks.shape[1]), F32),
        in_specs=[smem, smem, vmem, hbm, hbm],
        out_specs=vmem,
        scratch_shapes=[
            pltpu.VMEM(blocks.shape, BF16),
            pltpu.VMEM(start_basis.shape, BF16),
            pltpu.VMEM((64, 256), BF16),
            dma((2,)),
            pltpu.VMEM((NX, 64, 256), BF16),
            pltpu.VMEM((NX, 64, 256), BF16),
            pltpu.VMEM((NX, 64, 256), BF16),
            pltpu.VMEM((NX, 64, 256), BF16),
            pltpu.VMEM((NX, 2, 16, 256), F32),
            pltpu.VMEM((NZ // 2, 16, 256), BF16),
            pltpu.VMEM((2, NZ, 16, 256), BF16),
            pltpu.VMEM((NZ // 2, 16, 256), BF16),
            pltpu.VMEM((2, NF, 64, 256), BF16),
            pltpu.VMEM((2, NF, 16, 128), F32),
            dma((3,)), dma((3,)), dma((3,)), dma((3,)), dma((3,)), dma((3,)),
            dma((2, 15)), dma((2, 15)), dma((7,)), dma((7,)),
            dma((2, 7)), dma((2, 7)), dma((2, 7)), dma((2, 7)),
        ],
        compiler_params=pltpu.CompilerParams(collective_id=0, has_side_effects=True),
    )(annulus_of_block, ref_blocks, keep_mask, blocks, start_basis)


def solution(mesh):
    in_specs = (P("pix", "frm"), P("pix"), P(), P("pix", None), P(None, None, "frm"))
    out_specs = P("pix", None, None)
    return jax.shard_map(shards, mesh=mesh, in_specs=in_specs, out_specs=out_specs, check_vma=False)
```

```python
import functools

import jax
import jax.numpy as jnp
from jax import lax
from jax.experimental import pallas as pl
from jax.experimental.pallas import tpu as pltpu
from jax.sharding import PartitionSpec as P

ITERS = 4
ANNULI = 4
K = 32
NX = 4
NZ = 16
NF = 8
GROUP = 8
F32 = jnp.float32
BF16 = jnp.bfloat16
FRM_ORDER = (4, 3, 5, 2, 6, 1, 7)
BACK = (-4, 3, -3, 2, -2, 1, -1)
FAR_FIRST = (8, 7, 9, 6, 10, 5, 11, 4, 12, 3, 13, 2, 14, 1, 15)


def inverse_factors(gram):
    row_id = lax.broadcasted_iota(jnp.int32, (K, 128), 0)
    lane = lax.broadcasted_iota(jnp.int32, (K, 128), 1)
    first = (lane & 63) < K
    work = jnp.where(lane >= 64, jnp.where((lane & (K - 1)) == row_id, 1.0, 0.0), gram)
    scale = jnp.zeros((K, 128), F32)
    for start in range(0, K, GROUP):
        cols = [
            jnp.where(
                first,
                jnp.broadcast_to(work[:, j : j + 1], (K, 128)),
                jnp.broadcast_to(work[:, K + j : K + j + 1], (K, 128)),
            )
            for j in range(start, start + GROUP)
        ]
        for i in range(GROUP):
            j = start + i
            pivot = cols[i][j : j + 1, :]
            scale = jnp.where(row_id == j, jnp.broadcast_to(lax.rsqrt(pivot), (K, 128)), scale)
            if j < K - 1:
                ratio = jnp.where(row_id > j, cols[i], 0.0) * jnp.broadcast_to(1.0 / pivot, (K, 128))
                for m in range(i + 1, GROUP):
                    at = start + m
                    cols[m] = cols[m] - ratio * jnp.broadcast_to(cols[i][at : at + 1, :], (K, 128))
                work = work - ratio * jnp.broadcast_to(work[j : j + 1, :], (K, 128))
    return work * scale


def kernel(
    ann_ref, refs_ref, keep_ref, cur_hbm, sb_hbm, out_ref,
    cur_ref, sb_ref, mk, in_s, s4, xs, xr, xa, lab, zs, zr, zg, pr, gr,
    lab_s, lab_r, x1_s, x1_r, x2_s, x2_r, z1_s, z1_r, z2_s, z2_r, g_s, g_r, p_s, p_r,
):
    pix = lax.axis_index("pix")
    f = lax.axis_index("frm")
    x = pix // NZ
    z = lax.rem(pix, NZ)

    def x_peer(j):
        q = lax.rem(x + j, NX)
        return q, {"pix": q * NZ + z}

    def z_peer(j):
        q = lax.rem(z + j, NZ)
        return q, {"pix": x * NZ + q}

    def f_peer(j):
        return {"frm": lax.rem(f + j, NF)}

    def send(src, dst, s_sem, r_sem, peer):
        copy = pltpu.make_async_remote_copy(
            src_ref=src, dst_ref=dst, send_sem=s_sem, recv_sem=r_sem,
            device_id=peer, device_id_type=pl.DeviceIdType.MESH,
        )
        copy.start()
        return copy

    barrier = pltpu.get_barrier_semaphore()
    peers = [x_peer(j)[1] for j in range(1, NX)] + [z_peer(j)[1] for j in range(1, NZ)]
    peers += [f_peer(j) for j in range(1, NF)]
    for peer in peers:
        pl.semaphore_signal(barrier, inc=1, device_id=peer, device_id_type=pl.DeviceIdType.MESH)

    sb_copy = pltpu.make_async_copy(sb_hbm, sb_ref, in_s.at[0])
    cur_copy = pltpu.make_async_copy(cur_hbm, cur_ref, in_s.at[1])
    sb_copy.start()
    cur_copy.start()

    labels = [ann_ref[b] for b in range(2)]
    weights = []
    for b in range(2):
        hits = jnp.int32(0)
        for a in range(ANNULI):
            for r in range(8):
                same = (refs_ref[a, r] == pix * 2 + b) & (labels[b] == a)
                hits = jnp.maximum(hits, same.astype(jnp.int32))
        keep = keep_ref[b : b + 1, :]
        weights.append(jnp.where(keep == 1, jnp.full(keep.shape, hits).astype(F32), 0.0))
        lab[x, b] = jnp.full((16, 256), labels[b]).astype(F32)

    contract_last = (((1,), (1,)), ((), ()))

    def project(slot, spans):
        for b in range(2):
            part = lax.dot_general(spans[b], cur_ref[b], contract_last, preferred_element_type=F32)
            pr[slot, f, K * b : K * b + K, :] = part.astype(BF16)

    def send_projection(slot):
        return [
            send(pr.at[slot, f], pr.at[slot, f], p_s.at[slot, j - 1], p_r.at[slot, j - 1], f_peer(j))
            for j in FRM_ORDER
        ]

    def sum_projection(slot):
        raw = pr[slot, 0].astype(F32)
        for i in range(1, NF):
            raw = raw + pr[slot, i].astype(F32)
        return raw

    sb_copy.wait()
    spans = []
    for b in range(2):
        chosen = jnp.zeros((K, sb_ref.shape[2]), F32)
        for a in range(ANNULI):
            chosen = jnp.where(jnp.full(chosen.shape, labels[b]) == a, sb_ref[a].astype(F32), chosen)
        spans.append(chosen.astype(BF16))
    cur_copy.wait()
    project(0, spans)
    pl.semaphore_wait(barrier, len(peers))
    copies = send_projection(0)
    lab_copies = [
        send(lab.at[x], lab.at[x], lab_s.at[j - 1], lab_r.at[j - 1], x_peer(j)[1])
        for j in range(1, NX)
    ]
    for copy in copies:
        copy.wait_recv()
    raw = sum_projection(0)
    for b in range(2):
        mk[K * b : K * b + K, :] = (raw[K * b : K * b + K] * weights[b]).astype(BF16)
    for copy in lab_copies:
        copy.wait()
    for copy in copies:
        copy.wait_send()

    def step(t, carry):
        slot = lax.rem(t, 2)
        masked = [mk[K * b : K * b + K, :] for b in range(2)]

        def quarter(q, dst, at):
            lanes = pl.ds(pl.multiple_of(q * 256, 256), 256)
            for b in range(2):
                part = jnp.dot(masked[b], cur_ref[b, :, lanes], preferred_element_type=F32)
                dst[at, K * b : K * b + K, :] = part.astype(BF16)

        copies = []
        for j in (2, 1, 3):
            q, peer = x_peer(j)
            quarter(q, xs, q)
            copies.append(send(xs.at[q], xr.at[x], x1_s.at[j - 1], x1_r.at[j - 1], peer))
        quarter(x, xr, x)
        for copy in copies:
            copy.wait()
        for r in range(2):
            totals = [jnp.zeros((16, 256), F32) for _ in range(ANNULI)]
            for q in range(NX):
                for b in range(2):
                    value = xr[q, K * b + 16 * r : K * b + 16 * r + 16, :].astype(F32)
                    label = lab[q, b]
                    for a in range(ANNULI):
                        totals[a] = totals[a] + jnp.where(label == a, value, 0.0)
            for a in range(ANNULI):
                zs[2 * a + r] = totals[a].astype(BF16)
        mine = lax.rem(z, NZ // 2)
        copies = []
        for j in FAR_FIRST:
            q, peer = z_peer(j)
            part = zs.at[lax.rem(q, NZ // 2)]
            copies.append(
                send(part, zr.at[slot, z], z1_s.at[slot, j - 1], z1_r.at[slot, j - 1], peer)
            )
        zr[slot, z] = zs[mine]
        for copy in copies:
            copy.wait_recv()
        chunk = zr[slot, 0].astype(F32)
        for i in range(1, NZ):
            chunk = chunk + zr[slot, i].astype(F32)
        zg[mine] = chunk.astype(BF16)
        back = []
        for i, j in enumerate(BACK):
            peer = z_peer(j + NZ)[1]
            back.append(send(zg.at[mine], zg.at[mine], z2_s.at[i], z2_r.at[i], peer))
        for copy in back:
            copy.wait_recv()

        def pick(q, dst, at):
            for b in range(2):
                label = lab[q, b]
                for r in range(2):
                    value = jnp.zeros((16, 256), F32)
                    for a in range(ANNULI):
                        value = jnp.where(label == a, zg[2 * a + r].astype(F32), value)
                    dst[at, K * b + 16 * r : K * b + 16 * r + 16, :] = value.astype(BF16)

        last = []
        for j in (2, 1, 3):
            q, peer = x_peer(j)
            pick(q, xa, q)
            last.append(send(xa.at[q], s4.at[x], x2_s.at[j - 1], x2_r.at[j - 1], peer))
        pick(x, s4, x)
        for copy in copies + back:
            copy.wait_send()
        for copy in last:
            copy.wait()

        spans = [
            jnp.concatenate([s4[q, K * b : K * b + K, :] for q in range(NX)], axis=1)
            for b in range(2)
        ]
        grams = [
            lax.dot_general(s, s, contract_last, preferred_element_type=F32) for s in spans
        ]
        gr[slot, f] = jnp.concatenate(
            [g[16 * r : 16 * r + 16] for g in grams for r in range(2)], axis=1
        )
        g_copies = [
            send(gr.at[slot, f], gr.at[slot, f], g_s.at[slot, j - 1], g_r.at[slot, j - 1], f_peer(j))
            for j in FRM_ORDER
        ]
        project(slot, spans)
        p_copies = send_projection(slot)
        for copy in g_copies:
            copy.wait_recv()
        gram = gr[slot, 0]
        for i in range(1, NF):
            gram = gram + gr[slot, i]
        halves = [gram[:, K * i : K * i + K] for i in range(4)]
        gram = jnp.concatenate(
            [jnp.concatenate(halves[:2], axis=0), jnp.concatenate(halves[2:], axis=0),
             jnp.zeros((K, 64), F32)], axis=1
        )
        inverse = inverse_factors(gram)
        for copy in p_copies:
            copy.wait_recv()
        raw = sum_projection(slot)
        for b in range(2):
            proj = lax.dot_general(
                inverse[:, 64 + K * b : 64 + K * b + K], raw[K * b : K * b + K],
                (((1,), (0,)), ((), ())), precision=lax.Precision.HIGHEST,
                preferred_element_type=F32,
            )
            out_ref[b] = proj
            mk[K * b : K * b + K, :] = (proj * weights[b]).astype(BF16)
        for copy in g_copies + p_copies:
            copy.wait_send()
        return carry

    lax.fori_loop(1, ITERS + 1, step, 0)


def shards(curves, annulus_of_block, ref_blocks, keep_mask, start_basis):
    nblocks = annulus_of_block.shape[0]
    frames = curves.shape[1]
    blocks = curves.reshape(nblocks, -1, frames)
    vmem = pl.BlockSpec(memory_space=pltpu.VMEM)
    hbm = pl.BlockSpec(memory_space=pl.ANY)
    smem = pl.BlockSpec(memory_space=pltpu.SMEM)
    dma = pltpu.SemaphoreType.DMA
    return pl.pallas_call(
        kernel,
        out_shape=jax.ShapeDtypeStruct((nblocks, K, blocks.shape[1]), F32),
        in_specs=[smem, smem, vmem, hbm, hbm],
        out_specs=vmem,
        scratch_shapes=[
            pltpu.VMEM(blocks.shape, BF16),
            pltpu.VMEM(start_basis.shape, BF16),
            pltpu.VMEM((64, 256), BF16),
            dma((2,)),
            pltpu.VMEM((NX, 64, 256), BF16),
            pltpu.VMEM((NX, 64, 256), BF16),
            pltpu.VMEM((NX, 64, 256), BF16),
            pltpu.VMEM((NX, 64, 256), BF16),
            pltpu.VMEM((NX, 2, 16, 256), F32),
            pltpu.VMEM((NZ // 2, 16, 256), BF16),
            pltpu.VMEM((2, NZ, 16, 256), BF16),
            pltpu.VMEM((NZ // 2, 16, 256), BF16),
            pltpu.VMEM((2, NF, 64, 256), BF16),
            pltpu.VMEM((2, NF, 16, 128), F32),
            dma((3,)), dma((3,)), dma((3,)), dma((3,)), dma((3,)), dma((3,)),
            dma((2, 15)), dma((2, 15)), dma((7,)), dma((7,)),
            dma((2, 7)), dma((2, 7)), dma((2, 7)), dma((2, 7)),
        ],
        compiler_params=pltpu.CompilerParams(collective_id=0, has_side_effects=True),
    )(annulus_of_block, ref_blocks, keep_mask, blocks, start_basis)


def solution(mesh):
    in_specs = (P("pix", "frm"), P("pix"), P(), P("pix", None), P(None, None, "frm"))
    out_specs = P("pix", None, None)
    return jax.shard_map(shards, mesh=mesh, in_specs=in_specs, out_specs=out_specs, check_vma=False)
```

```python
import functools

import jax
import jax.numpy as jnp
from jax import lax
from jax.experimental import pallas as pl
from jax.experimental.pallas import tpu as pltpu
from jax.sharding import PartitionSpec as P

ITERS = 4
ANNULI = 4
K = 32
NX = 4
NZ = 16
NF = 8
GROUP = 8
F32 = jnp.float32
BF16 = jnp.bfloat16
FRM_ORDER = (4, 3, 5, 2, 6, 1, 7)
BACK = sorted(
    [(i, d) for i in range(NX) for d in range(-4, 4) if (i, d) != (0, 0)],
    key=lambda o: (-min(o[0], NX - o[0]) - abs(o[1]), o),
)
FAR_FIRST = (8, 7, 9, 6, 10, 5, 11, 4, 12, 3, 13, 2, 14, 1, 15)


def inverse_factors(gram):
    row_id = lax.broadcasted_iota(jnp.int32, (K, 128), 0)
    lane = lax.broadcasted_iota(jnp.int32, (K, 128), 1)
    first = (lane & 63) < K
    work = jnp.where(lane >= 64, jnp.where((lane & (K - 1)) == row_id, 1.0, 0.0), gram)
    scale = jnp.zeros((K, 128), F32)
    for start in range(0, K, GROUP):
        cols = [
            jnp.where(
                first,
                jnp.broadcast_to(work[:, j : j + 1], (K, 128)),
                jnp.broadcast_to(work[:, K + j : K + j + 1], (K, 128)),
            )
            for j in range(start, start + GROUP)
        ]
        for i in range(GROUP):
            j = start + i
            pivot = cols[i][j : j + 1, :]
            scale = jnp.where(row_id == j, jnp.broadcast_to(lax.rsqrt(pivot), (K, 128)), scale)
            if j < K - 1:
                ratio = jnp.where(row_id > j, cols[i], 0.0) * jnp.broadcast_to(1.0 / pivot, (K, 128))
                for m in range(i + 1, GROUP):
                    at = start + m
                    cols[m] = cols[m] - ratio * jnp.broadcast_to(cols[i][at : at + 1, :], (K, 128))
                work = work - ratio * jnp.broadcast_to(work[j : j + 1, :], (K, 128))
    return work * scale


def kernel(
    ann_ref, refs_ref, keep_ref, cur_hbm, sb_hbm, out_ref,
    cur_ref, sb_ref, mk, in_s, xs, xr, lab, zs, zr, zg, pr, gr,
    lab_s, lab_r, x1_s, x1_r, z1_s, z1_r, z2_s, z2_r, g_s, g_r, p_s, p_r,
):
    pix = lax.axis_index("pix")
    f = lax.axis_index("frm")
    x = pix // NZ
    z = lax.rem(pix, NZ)

    def x_peer(j):
        q = lax.rem(x + j, NX)
        return q, {"pix": q * NZ + z}

    def z_peer(j):
        q = lax.rem(z + j, NZ)
        return q, {"pix": x * NZ + q}

    def back_peer(i, d):
        return {"pix": lax.rem(x + i, NX) * NZ + lax.rem(z + d + NZ, NZ)}

    def f_peer(j):
        return {"frm": lax.rem(f + j, NF)}

    def send(src, dst, s_sem, r_sem, peer):
        copy = pltpu.make_async_remote_copy(
            src_ref=src, dst_ref=dst, send_sem=s_sem, recv_sem=r_sem,
            device_id=peer, device_id_type=pl.DeviceIdType.MESH,
        )
        copy.start()
        return copy

    barrier = pltpu.get_barrier_semaphore()
    peers = [x_peer(j)[1] for j in range(1, NX)] + [z_peer(j)[1] for j in range(1, NZ)]
    peers += [back_peer(i, d) for i in range(1, NX) for d in range(-4, 5) if d != 0]
    peers += [f_peer(j) for j in range(1, NF)]
    for peer in peers:
        pl.semaphore_signal(barrier, inc=1, device_id=peer, device_id_type=pl.DeviceIdType.MESH)

    sb_copy = pltpu.make_async_copy(sb_hbm, sb_ref, in_s.at[0])
    cur_copy = pltpu.make_async_copy(cur_hbm, cur_ref, in_s.at[1])
    sb_copy.start()
    cur_copy.start()

    labels = [ann_ref[b] for b in range(2)]
    weights = []
    for b in range(2):
        hits = jnp.int32(0)
        for a in range(ANNULI):
            for r in range(8):
                same = (refs_ref[a, r] == pix * 2 + b) & (labels[b] == a)
                hits = jnp.maximum(hits, same.astype(jnp.int32))
        keep = keep_ref[b : b + 1, :]
        weights.append(jnp.where(keep == 1, jnp.full(keep.shape, hits).astype(F32), 0.0))
        lab[x, b] = jnp.full((16, 256), labels[b]).astype(F32)

    contract_last = (((1,), (1,)), ((), ()))

    def project(slot, spans):
        for b in range(2):
            part = lax.dot_general(spans[b], cur_ref[b], contract_last, preferred_element_type=F32)
            pr[slot, f, K * b : K * b + K, :] = part.astype(BF16)

    def send_projection(slot):
        return [
            send(pr.at[slot, f], pr.at[slot, f], p_s.at[slot, j - 1], p_r.at[slot, j - 1], f_peer(j))
            for j in FRM_ORDER
        ]

    def sum_projection(slot):
        raw = pr[slot, 0].astype(F32)
        for i in range(1, NF):
            raw = raw + pr[slot, i].astype(F32)
        return raw

    sb_copy.wait()
    spans = []
    for b in range(2):
        chosen = jnp.zeros((K, sb_ref.shape[2]), F32)
        for a in range(ANNULI):
            chosen = jnp.where(jnp.full(chosen.shape, labels[b]) == a, sb_ref[a].astype(F32), chosen)
        spans.append(chosen.astype(BF16))
    cur_copy.wait()
    project(0, spans)
    pl.semaphore_wait(barrier, len(peers))
    copies = send_projection(0)
    lab_copies = [
        send(lab.at[x], lab.at[x], lab_s.at[j - 1], lab_r.at[j - 1], x_peer(j)[1])
        for j in range(1, NX)
    ]
    for copy in copies:
        copy.wait_recv()
    raw = sum_projection(0)
    for b in range(2):
        mk[K * b : K * b + K, :] = (raw[K * b : K * b + K] * weights[b]).astype(BF16)
    for copy in lab_copies:
        copy.wait()
    for copy in copies:
        copy.wait_send()

    def step(t, carry):
        slot = lax.rem(t, 2)
        masked = [mk[K * b : K * b + K, :] for b in range(2)]

        def quarter(q, dst, at):
            lanes = pl.ds(pl.multiple_of(q * 256, 256), 256)
            for b in range(2):
                part = jnp.dot(masked[b], cur_ref[b, :, lanes], preferred_element_type=F32)
                dst[at, K * b : K * b + K, :] = part.astype(BF16)

        copies = []
        for j in (2, 1, 3):
            q, peer = x_peer(j)
            quarter(q, xs, q)
            copies.append(send(xs.at[q], xr.at[x], x1_s.at[j - 1], x1_r.at[j - 1], peer))
        quarter(x, xr, x)
        for copy in copies:
            copy.wait()
        for r in range(2):
            totals = [jnp.zeros((16, 256), F32) for _ in range(ANNULI)]
            for q in range(NX):
                for b in range(2):
                    value = xr[q, K * b + 16 * r : K * b + 16 * r + 16, :].astype(F32)
                    label = lab[q, b]
                    for a in range(ANNULI):
                        totals[a] = totals[a] + jnp.where(label == a, value, 0.0)
            for a in range(ANNULI):
                zs[2 * a + r] = totals[a].astype(BF16)
        mine = lax.rem(z, NZ // 2)
        copies = []
        for j in FAR_FIRST:
            q, peer = z_peer(j)
            part = zs.at[lax.rem(q, NZ // 2)]
            copies.append(
                send(part, zr.at[slot, z], z1_s.at[slot, j - 1], z1_r.at[slot, j - 1], peer)
            )
        zr[slot, z] = zs[mine]
        for copy in copies:
            copy.wait_recv()
        chunk = zr[slot, 0].astype(F32)
        for i in range(1, NZ):
            chunk = chunk + zr[slot, i].astype(F32)
        zg[x, mine] = chunk.astype(BF16)
        back = []
        for i, (dx, dz) in enumerate(BACK):
            peer = back_peer(dx, dz)
            back.append(send(zg.at[x, mine], zg.at[x, mine], z2_s.at[i], z2_r.at[i], peer))
        for copy in copies:
            copy.wait_send()
        for copy in back:
            copy.wait_recv()

        def pick(q, b):
            label = jnp.full((16, 256), labels[b])
            halves = []
            for r in range(2):
                value = zg[q, r].astype(F32)
                for a in range(1, ANNULI):
                    value = jnp.where(label == a, zg[q, 2 * a + r].astype(F32), value)
                halves.append(value.astype(BF16))
            return jnp.concatenate(halves, axis=0)

        spans = [jnp.concatenate([pick(q, b) for q in range(NX)], axis=1) for b in range(2)]
        grams = [
            lax.dot_general(s, s, contract_last, preferred_element_type=F32) for s in spans
        ]
        gr[slot, f] = jnp.concatenate(
            [g[16 * r : 16 * r + 16] for g in grams for r in range(2)], axis=1
        )
        g_copies = [
            send(gr.at[slot, f], gr.at[slot, f], g_s.at[slot, j - 1], g_r.at[slot, j - 1], f_peer(j))
            for j in FRM_ORDER
        ]
        project(slot, spans)
        p_copies = send_projection(slot)
        for copy in g_copies:
            copy.wait_recv()
        gram = gr[slot, 0]
        for i in range(1, NF):
            gram = gram + gr[slot, i]
        halves = [gram[:, K * i : K * i + K] for i in range(4)]
        gram = jnp.concatenate(
            [jnp.concatenate(halves[:2], axis=0), jnp.concatenate(halves[2:], axis=0),
             jnp.zeros((K, 64), F32)], axis=1
        )
        inverse = inverse_factors(gram)
        for copy in p_copies:
            copy.wait_recv()
        raw = sum_projection(slot)
        for b in range(2):
            proj = lax.dot_general(
                inverse[:, 64 + K * b : 64 + K * b + K], raw[K * b : K * b + K],
                (((1,), (0,)), ((), ())), precision=lax.Precision.HIGHEST,
                preferred_element_type=F32,
            )
            out_ref[b] = proj
            mk[K * b : K * b + K, :] = (proj * weights[b]).astype(BF16)
        for copy in back + g_copies + p_copies:
            copy.wait_send()
        return carry

    lax.fori_loop(1, ITERS + 1, step, 0)


def shards(curves, annulus_of_block, ref_blocks, keep_mask, start_basis):
    nblocks = annulus_of_block.shape[0]
    frames = curves.shape[1]
    blocks = curves.reshape(nblocks, -1, frames)
    vmem = pl.BlockSpec(memory_space=pltpu.VMEM)
    hbm = pl.BlockSpec(memory_space=pl.ANY)
    smem = pl.BlockSpec(memory_space=pltpu.SMEM)
    dma = pltpu.SemaphoreType.DMA
    return pl.pallas_call(
        kernel,
        out_shape=jax.ShapeDtypeStruct((nblocks, K, blocks.shape[1]), F32),
        in_specs=[smem, smem, vmem, hbm, hbm],
        out_specs=vmem,
        scratch_shapes=[
            pltpu.VMEM(blocks.shape, BF16),
            pltpu.VMEM(start_basis.shape, BF16),
            pltpu.VMEM((64, 256), BF16),
            dma((2,)),
            pltpu.VMEM((NX, 64, 256), BF16),
            pltpu.VMEM((NX, 64, 256), BF16),
            pltpu.VMEM((NX, 2, 16, 256), F32),
            pltpu.VMEM((NZ // 2, 16, 256), BF16),
            pltpu.VMEM((2, NZ, 16, 256), BF16),
            pltpu.VMEM((NX, NZ // 2, 16, 256), BF16),
            pltpu.VMEM((2, NF, 64, 256), BF16),
            pltpu.VMEM((2, NF, 16, 128), F32),
            dma((3,)), dma((3,)), dma((3,)), dma((3,)),
            dma((2, 15)), dma((2, 15)), dma((31,)), dma((31,)),
            dma((2, 7)), dma((2, 7)), dma((2, 7)), dma((2, 7)),
        ],
        compiler_params=pltpu.CompilerParams(collective_id=0, has_side_effects=True),
    )(annulus_of_block, ref_blocks, keep_mask, blocks, start_basis)


def solution(mesh):
    in_specs = (P("pix", "frm"), P("pix"), P(), P("pix", None), P(None, None, "frm"))
    out_specs = P("pix", None, None)
    return jax.shard_map(shards, mesh=mesh, in_specs=in_specs, out_specs=out_specs, check_vma=False)
```
